32 devices in a mesh: var: 8 (over y, x, core), samp: 4 (over z).
Axes of the slice: x: 2, y: 2, z: 4, core: 2. Of those that a mesh axis runs over, the one named last changes fastest.
Arguments:
- dosages: bfloat16 [16384, 4096], P('samp', 'var'), as said below
- window_end: int32 [4096], P('var'), may hold values from 0 to 4095, as said below
Outputs:
- correlations: bfloat16 [4096, 2048], P('var')
The draws below stay inside these ranges and needn't reach their ends.
Inputs may be any that keep to these rules, and one draw needn't show every extreme that they name: For a variant in block b (of 512 variants), window_end lies in block b + 1, b + 2 or b + 3 (the same block reach for the whole block), clipped to 4095; some variant reaches the last variant of the block three ahead. `dosages`: dosages lie between 0 and 2.
All inputs are finite; a program needn't handle non-finite values.
Results may differ from the reference program's by a relative error of at most 0.0034.
Values may be sent and summed in bfloat16 or wider, within the bound.
A program may use at most 64 MiB of HBM per device.

```python
import jax
import jax.numpy as jnp
from jax import lax

VB = 512
S_DEV = 4096
N_VAR = 8
N_SAMP = 4


def draw_dosages(key, part):
    total = S_DEV * N_SAMP
    count = VB * N_VAR
    key_freq, key_noise = jax.random.split(key, 2)
    freq = jnp.exp(jax.random.uniform(key_freq, (count,), jnp.float32, jnp.log(0.02), jnp.log(0.5)))
    ramp = 0.4 + 1.2 * jnp.arange(total, dtype=jnp.float32) / total
    noise = jax.random.normal(key_noise, (total, count), jnp.float32)
    base = 2.0 * freq[None, :] * ramp[:, None]
    values = base + 0.6 * jnp.sqrt(freq)[None, :] * noise
    return jnp.clip(values, 0.0, 2.0).astype(jnp.bfloat16)


def draw_window_end(key, part):
    count = VB * N_VAR
    key_reach, key_offset = jax.random.split(key)
    reach = jax.random.randint(key_reach, (N_VAR,), 1, 4, jnp.int32)
    reach = reach.at[0].set(3)
    offset = jax.random.randint(key_offset, (N_VAR, VB), 0, VB, jnp.int32)
    offset = offset.at[:, 0].set(VB - 1)
    block = jnp.arange(N_VAR, dtype=jnp.int32)
    ends = (block[:, None] + reach[:, None]) * VB + offset
    return jnp.minimum(ends, count - 1).reshape(count).astype(jnp.int32)


def setup_inputs(seed: int = 0) -> dict:
    key_of = jax.random.split(jax.random.key(seed), 3)
    return {
        "dosages": draw_dosages(jax.random.fold_in(key_of[2], 71), 0),
        "window_end": draw_window_end(jax.random.fold_in(key_of[2], 71), 0),
    }


def reference(dosages, window_end):
    total = dosages.shape[0]
    count = dosages.shape[1]
    data = dosages.astype(jnp.float32)
    mean = lax.optimization_barrier(jnp.sum(data, axis=0)) / total
    square = lax.optimization_barrier(jnp.sum(data * data, axis=0)) / total
    spread = 1.0 / jnp.sqrt(square - mean * mean + 1e-05)
    standard = ((data - mean[None, :]) * spread[None, :]).astype(jnp.bfloat16)
    padded = jnp.concatenate([standard, jnp.zeros((total, 3 * VB), jnp.bfloat16)], axis=1)
    columns = jnp.arange(4 * VB, dtype=jnp.int32)

    def one_block(block):
        start = (block * VB).astype(jnp.int32)
        own = lax.dynamic_slice_in_dim(padded, start, VB, 1)
        band = lax.dynamic_slice_in_dim(padded, start, 4 * VB, 1)
        gram = jnp.dot(own.T, band, preferred_element_type=jnp.float32)
        ends = lax.dynamic_slice_in_dim(window_end, start, VB, 0)
        target = start + columns
        keep = (columns[None, :] < VB) | (target[None, :] <= ends[:, None])
        return jnp.where(keep, gram / total, 0.0).astype(jnp.bfloat16)
    blocks = lax.map(one_block, jnp.arange(count // VB, dtype=jnp.int32))
    return blocks.reshape(count, 4 * VB)
```

```python
import functools

import jax
import jax.numpy as jnp
from jax import lax
from jax.experimental import pallas as pl
from jax.experimental.pallas import tpu as pltpu
from jax.sharding import PartitionSpec as P

MESH = pl.DeviceIdType.MESH
REACH = 4
PARTS = 4
SUBS = 4


def kernel(
    total, nv, ns, data, out, x, xt, other, stat, mine, give, got, arrived, result,
    stat_send, stat_recv, swap_send, swap_recv, near_send, far_send, pass_send, third_send,
    near_recv, far_recv, third_recv, give_send, give_recv,
    sum_send, sum_recv, back_send, back_recv, out_sem,
):
    v = lax.axis_index("var")
    s = lax.axis_index("samp")
    rows, width = data.shape
    half = rows // 2
    chips = nv // 2
    c = v // 2
    j = v % 2
    tile = min(256, half)
    part = half // PARTS

    def dev(chip, core, group):
        return {"var": chip * 2 + core, "samp": group}

    def remote(src, dst, send, recv, where):
        return pltpu.make_async_remote_copy(
            src_ref=src, dst_ref=dst, send_sem=send, recv_sem=recv,
            device_id=where, device_id_type=MESH,
        )

    barrier = pltpu.get_barrier_semaphore()

    def greet(where):
        pl.semaphore_signal(barrier, inc=1, device_id=where, device_id_type=MESH)

    greet(dev(c, 1 - j, s))
    for off in range(1, ns):
        greet(dev(c, j, lax.rem(s + off, ns)))
    for off in (-2, -1, 1, 2):
        @pl.when((c + off >= 0) & (c + off < chips))
        def _():
            greet(dev(c + off, j, s))

    def add_up(i, carry):
        a, b = carry
        d = data[pl.ds(pl.multiple_of(i * tile, tile), tile), :].astype(jnp.float32)
        d = d.reshape(tile // 8, 8, width)
        return a + jnp.sum(d, axis=0), b + jnp.sum(d * d, axis=0)

    zero = jnp.zeros((8, width), jnp.float32)
    a, b = lax.fori_loop(0, rows // tile, add_up, (zero, zero))
    stat[s, 0:1, :] = jnp.sum(a, axis=0, keepdims=True)
    stat[s, 1:2, :] = jnp.sum(b, axis=0, keepdims=True)

    peers = jnp.int32(ns)
    for off in (-2, -1, 1, 2):
        peers = peers + ((c + off >= 0) & (c + off < chips)).astype(jnp.int32)
    pl.semaphore_wait(barrier, peers)

    def stat_out(off):
        return remote(stat.at[s], stat.at[s], stat_send.at[off], stat_recv.at[s],
                      dev(c, j, lax.rem(s + off, ns)))

    for off in range(1, ns):
        stat_out(off).start()
    for off in range(1, ns):
        src = lax.rem(s + off, ns)
        remote(stat.at[src], stat.at[src], stat_send.at[off], stat_recv.at[src],
               dev(c, j, src)).wait_recv()
    sums = stat[0, 0:1, :]
    squares = stat[0, 1:2, :]
    for g in range(1, ns):
        sums = sums + stat[g, 0:1, :]
        squares = squares + stat[g, 1:2, :]
    mean = sums / total
    spread = 1.0 / jnp.sqrt(squares / total - mean * mean + 1e-05)

    def standard(start):
        d = data[pl.ds(pl.multiple_of(start, tile), tile), :].astype(jnp.float32)
        return ((d - mean) * spread).astype(jnp.bfloat16)

    @pl.loop(0, half // tile)
    def _(i):
        at = pl.multiple_of(i * tile, tile)
        other[pl.ds(at, tile), :] = standard((1 - j) * half + at)

    swap = remote(other, x.at[j], swap_send, swap_recv, dev(c, 1 - j, s))
    swap.start()

    @pl.loop(0, half // tile)
    def _(i):
        at = pl.multiple_of(i * tile, tile)
        x[j, pl.ds(at, tile), :] = standard(j * half + at)

    for slot, reach in ((2, 1), (3, 1), (4, 2)):
        @pl.when(c + reach >= chips)
        def _():
            @pl.loop(0, half // tile)
            def _(i):
                at = pl.multiple_of(i * tile, tile)
                x[slot, pl.ds(at, tile), :] = jnp.zeros((tile, width), jnp.bfloat16)

    remote(other, x.at[1 - j], swap_send, swap_recv, dev(c, 1 - j, s)).wait_recv()

    def piece(slot, q):
        return x.at[slot, pl.ds(q * part, part), :]

    def near(q):
        return remote(piece(0, q), piece(2, q), near_send.at[q], near_recv.at[q], dev(c - 1, j, s))

    def far(q):
        return remote(piece(0, q), piece(4, q), far_send.at[q], far_recv.at[q], dev(c - 2, j, s))

    def passed(q):
        return remote(piece(4, q), piece(2, q), pass_send.at[q], near_recv.at[q], dev(c + 1, j, s))

    def third():
        return remote(x.at[1], x.at[3], third_send, third_recv, dev(c - 1, j, s))

    odd = c % 2 == 1
    has_far = c >= 2
    has_near = (c >= 1) & odd
    relays = (c % 2 == 0) & (c + 2 < chips)

    @pl.when(has_far)
    def _():
        for q in range(PARTS):
            far(q).start()

    @pl.when(has_near)
    def _():
        for q in range(PARTS):
            near(q).start()

    @pl.when(c >= 1)
    def _():
        third().start()

    def take_far(q):
        @pl.when(c + 2 < chips)
        def _():
            remote(piece(0, q), piece(4, q), far_send.at[q], far_recv.at[q],
                   dev(c + 2, j, s)).wait_recv()

        @pl.when(relays)
        def _():
            passed(q).start()

    def take_near():
        @pl.when(c + 1 < chips)
        def _():
            for q in range(PARTS):
                remote(piece(0, q), piece(2, q), near_send.at[q], near_recv.at[q],
                       dev(c + 1, j, s)).wait_recv()

    def take_third():
        @pl.when(c + 1 < chips)
        def _():
            remote(x.at[1], x.at[3], third_send, third_recv, dev(c + 1, j, s)).wait_recv()

    for r in range(2):
        @pl.loop(0, half // tile)
        def _(i):
            at = pl.multiple_of(i * tile, tile)
            xt[r, :, pl.ds(at, tile)] = x[r, pl.ds(at, tile), :].T

    side = min(256, width)
    slots = ((0, 1), (1, 2), (2, 4), (3, 3))
    column = ((0, 0), (1, 1), (2, 3), (3, 2))

    def pick(pair, r):
        return pair[0] + r * (pair[1] - pair[0])

    def product(t, r, into):
        slot = pick(slots[t], r)

        @pl.loop(0, (width // side) ** 2)
        def _(i):
            top = pl.multiple_of((i // (width // side)) * side, side)
            left = pl.multiple_of((i % (width // side)) * side, side)
            into[t, pl.ds(top, side), pl.ds(left, side)] = jnp.dot(
                xt[r, pl.ds(top, side), :], x[slot, :, pl.ds(left, side)],
                preferred_element_type=jnp.float32,
            )

    def gave(t):
        return remote(give.at[t], got.at[t], give_send.at[t], give_recv.at[t], dev(c, 1 - j, s))

    def grams(t):
        product(t, 1 - j, give)
        gave(t).start()
        product(t, j, mine)
        gave(t).wait_recv()

    block = width // 2 // SUBS

    def chain(n):
        way = n % 2
        u = n // 2
        lines = pl.ds(pl.multiple_of(way * (width // 2) + u * block, block), block)
        first = s == way * (ns - 1)
        last = s == (1 - way) * (ns - 1)
        step = 1 - 2 * way
        return lines, first, last, step

    def place(t):
        return pl.ds(pl.multiple_of(pick(column[t], j) * width, width), width)

    def to_sum(t, n, group):
        lines = chain(n)[0]
        return remote(mine.at[t, lines, :], arrived.at[t, lines, :], sum_send.at[t, n],
                      sum_recv.at[t, n], dev(c, j, group))

    def to_back(t, n, group):
        lines = chain(n)[0]
        spot = result.at[lines, place(t)]
        return remote(spot, spot, back_send.at[t, n], back_recv.at[t, n], dev(c, j, group))

    def reduce(t):
        @pl.loop(0, 2 * SUBS)
        def _(n):
            lines, first, last, step = chain(n)
            mine[t, lines, :] = mine[t, lines, :] + got[t, lines, :]

            @pl.when(jnp.logical_not(first))
            def _():
                to_sum(t, n, s - step).wait_recv()
                mine[t, lines, :] = mine[t, lines, :] + arrived[t, lines, :]

            @pl.when(jnp.logical_not(last))
            def _():
                to_sum(t, n, s + step).start()

            @pl.when(last)
            def _():
                result[lines, place(t)] = (mine[t, lines, :] / total).astype(jnp.bfloat16)
                to_back(t, n, s - step).start()

    def finish(t):
        @pl.loop(0, 2 * SUBS)
        def _(n):
            lines, first, last, step = chain(n)

            @pl.when(jnp.logical_not(last))
            def _():
                to_back(t, n, s + step).wait_recv()

                @pl.when(jnp.logical_not(first))
                def _():
                    to_back(t, n, s - step).start()

        store(t).start()

    def store(t):
        return pltpu.make_async_copy(result.at[:, place(t)], out.at[:, place(t)], out_sem.at[t])

    grams(0)
    reduce(0)
    take_far(0)
    finish(0)
    for q in range(1, PARTS):
        take_far(q)
    take_near()
    grams(1)
    reduce(1)
    grams(2)
    reduce(2)
    finish(1)
    take_third()
    grams(3)
    reduce(3)
    finish(2)
    finish(3)

    for off in range(1, ns):
        stat_out(off).wait_send()
    swap.wait_send()

    @pl.when(has_far)
    def _():
        for q in range(PARTS):
            far(q).wait_send()

    @pl.when(has_near)
    def _():
        for q in range(PARTS):
            near(q).wait_send()

    @pl.when(c >= 1)
    def _():
        third().wait_send()

    @pl.when(relays)
    def _():
        for q in range(PARTS):
            passed(q).wait_send()

    for t in range(REACH):
        gave(t).wait_send()
        store(t).wait()

        @pl.loop(0, 2 * SUBS)
        def _(n):
            lines, first, last, step = chain(n)

            @pl.when(jnp.logical_not(last))
            def _():
                to_sum(t, n, s + step).wait_send()

            @pl.when(jnp.logical_not(first))
            def _():
                to_back(t, n, s - step).wait_send()


def per_device(nv, ns, dosages, window_end):
    rows, width = dosages.shape
    half = rows // 2
    dma = pltpu.SemaphoreType.DMA
    f32, bf16 = jnp.float32, jnp.bfloat16
    raw = pl.pallas_call(
        functools.partial(kernel, rows * ns, nv, ns),
        out_shape=jax.ShapeDtypeStruct((width, REACH * width), bf16),
        in_specs=[pl.BlockSpec(memory_space=pltpu.VMEM)],
        out_specs=pl.BlockSpec(memory_space=pl.ANY),
        scratch_shapes=[
            pltpu.VMEM((REACH + 1, half, width), bf16),
            pltpu.VMEM((2, width, half), bf16),
            pltpu.VMEM((half, width), bf16),
            pltpu.VMEM((ns, 8, width), f32),
            pltpu.VMEM((REACH, width, width), f32),
            pltpu.VMEM((REACH, width, width), f32),
            pltpu.VMEM((REACH, width, width), f32),
            pltpu.VMEM((REACH, width, width), f32),
            pltpu.VMEM((width, REACH * width), bf16),
            dma((ns,)), dma((ns,)), dma(()), dma(()),
            dma((PARTS,)), dma((PARTS,)), dma((PARTS,)), dma(()),
            dma((PARTS,)), dma((PARTS,)), dma(()), dma((REACH,)), dma((REACH,)),
            dma((REACH, 2 * SUBS)), dma((REACH, 2 * SUBS)),
            dma((REACH, 2 * SUBS)), dma((REACH, 2 * SUBS)), dma((REACH,)),
        ],
        compiler_params=pltpu.CompilerParams(
            collective_id=0, has_side_effects=True, vmem_limit_bytes=60 * 1024 * 1024
        ),
    )(dosages)
    columns = jnp.arange(REACH * width, dtype=jnp.int32)
    target = lax.axis_index("var") * width + columns
    keep = (columns[None, :] < width) | (target[None, :] <= window_end[:, None])
    return jnp.where(keep, raw, jnp.zeros((), bf16))


def solution(mesh):
    placed = (P("samp", "var"), P("var"))
    return jax.shard_map(
        functools.partial(per_device, mesh.shape["var"], mesh.shape["samp"]),
        mesh=mesh, in_specs=placed, out_specs=P("var", None), check_vma=False,
    )
```

```python
import functools

import jax
import jax.numpy as jnp
from jax import lax
from jax.experimental import pallas as pl
from jax.experimental.pallas import tpu as pltpu
from jax.sharding import PartitionSpec as P

MESH = pl.DeviceIdType.MESH
REACH = 4
PARTS = 4
SUBS = 4
SLACK = 1
PACE = 3


def kernel(
    total, nv, ns, data, out, x, xt, other, stat, mine, give, got, arrived, result,
    stat_send, stat_recv, swap_send, swap_recv, near_send, far_send, pass_send, third_send,
    near_recv, far_recv, third_recv, give_send, give_recv,
    sum_send, sum_recv, back_send, back_recv, out_sem,
):
    v = lax.axis_index("var")
    s = lax.axis_index("samp")
    rows, width = data.shape
    half = rows // 2
    chips = nv // 2
    c = v // 2
    j = v % 2
    tile = min(256, half)
    part = half // PARTS

    def dev(chip, core, group):
        return {"var": chip * 2 + core, "samp": group}

    def remote(src, dst, send, recv, where):
        return pltpu.make_async_remote_copy(
            src_ref=src, dst_ref=dst, send_sem=send, recv_sem=recv,
            device_id=where, device_id_type=MESH,
        )

    barrier = pltpu.get_barrier_semaphore()

    def greet(where):
        pl.semaphore_signal(barrier, inc=1, device_id=where, device_id_type=MESH)

    greet(dev(c, 1 - j, s))
    for off in range(1, ns):
        greet(dev(c, j, lax.rem(s + off, ns)))
    for off in (-2, -1, 1, 2):
        @pl.when((c + off >= 0) & (c + off < chips))
        def _():
            greet(dev(c + off, j, s))

    def add_up(i, carry):
        a, b = carry
        d = data[pl.ds(pl.multiple_of(i * tile, tile), tile), :].astype(jnp.float32)
        d = d.reshape(tile // 8, 8, width)
        return a + jnp.sum(d, axis=0), b + jnp.sum(d * d, axis=0)

    zero = jnp.zeros((8, width), jnp.float32)
    a, b = lax.fori_loop(0, rows // tile, add_up, (zero, zero))
    stat[s, 0:1, :] = jnp.sum(a, axis=0, keepdims=True)
    stat[s, 1:2, :] = jnp.sum(b, axis=0, keepdims=True)

    peers = jnp.int32(ns)
    for off in (-2, -1, 1, 2):
        peers = peers + ((c + off >= 0) & (c + off < chips)).astype(jnp.int32)
    pl.semaphore_wait(barrier, peers)

    def stat_out(off):
        return remote(stat.at[s], stat.at[s], stat_send.at[off], stat_recv.at[s],
                      dev(c, j, lax.rem(s + off, ns)))

    for off in range(1, ns):
        stat_out(off).start()
    for off in range(1, ns):
        src = lax.rem(s + off, ns)
        remote(stat.at[src], stat.at[src], stat_send.at[off], stat_recv.at[src],
               dev(c, j, src)).wait_recv()
    sums = stat[0, 0:1, :]
    squares = stat[0, 1:2, :]
    for g in range(1, ns):
        sums = sums + stat[g, 0:1, :]
        squares = squares + stat[g, 1:2, :]
    mean = sums / total
    spread = 1.0 / jnp.sqrt(squares / total - mean * mean + 1e-05)

    def standard(start):
        d = data[pl.ds(pl.multiple_of(start, tile), tile), :].astype(jnp.float32)
        return ((d - mean) * spread).astype(jnp.bfloat16)

    @pl.loop(0, half // tile)
    def _(i):
        at = pl.multiple_of(i * tile, tile)
        other[pl.ds(at, tile), :] = standard((1 - j) * half + at)

    swap = remote(other, x.at[j], swap_send, swap_recv, dev(c, 1 - j, s))
    swap.start()

    @pl.loop(0, half // tile)
    def _(i):
        at = pl.multiple_of(i * tile, tile)
        x[j, pl.ds(at, tile), :] = standard(j * half + at)

    for slot, reach in ((2, 1), (3, 1), (4, 2)):
        @pl.when(c + reach >= chips)
        def _():
            @pl.loop(0, half // tile)
            def _(i):
                at = pl.multiple_of(i * tile, tile)
                x[slot, pl.ds(at, tile), :] = jnp.zeros((tile, width), jnp.bfloat16)

    remote(other, x.at[1 - j], swap_send, swap_recv, dev(c, 1 - j, s)).wait_recv()

    def piece(slot, q):
        return x.at[slot, pl.ds(pl.multiple_of(q * part, part), part), :]

    def near(q):
        return remote(piece(0, q), piece(2, q), near_send.at[q], near_recv.at[q], dev(c - 1, j, s))

    def far(q):
        return remote(piece(0, q), piece(4, q), far_send.at[q], far_recv.at[q], dev(c - 2, j, s))

    def passed(q):
        return remote(piece(4, q), piece(2, q), pass_send.at[q], near_recv.at[q], dev(c + 1, j, s))

    def third():
        return remote(x.at[1], x.at[3], third_send, third_recv, dev(c - 1, j, s))

    odd = c % 2 == 1
    has_far = c >= 2
    has_near = (c >= 1) & odd
    relays = (c % 2 == 0) & (c + 2 < chips)

    @pl.when(has_far)
    def _():
        for q in range(PARTS):
            far(q).start()

    @pl.when(has_near)
    def _():
        for q in range(PARTS):
            near(q).start()

    @pl.when(c >= 1)
    def _():
        third().start()

    def far_here(q):
        return remote(piece(0, q), piece(4, q), far_send.at[q], far_recv.at[q], dev(c + 2, j, s))

    def relay(q):
        @pl.when(relays)
        def _():
            far_here(q).wait_recv()
            passed(q).start()

    def take_far():
        @pl.when((c + 2 < chips) & odd)
        def _():
            for q in range(PARTS):
                far_here(q).wait_recv()

    def take_near():
        @pl.when(c + 1 < chips)
        def _():
            for q in range(PARTS):
                remote(piece(0, q), piece(2, q), near_send.at[q], near_recv.at[q],
                       dev(c + 1, j, s)).wait_recv()

    def take_third():
        @pl.when(c + 1 < chips)
        def _():
            remote(x.at[1], x.at[3], third_send, third_recv, dev(c + 1, j, s)).wait_recv()

    for r in range(2):
        @pl.loop(0, half // tile)
        def _(i):
            at = pl.multiple_of(i * tile, tile)
            xt[r, :, pl.ds(at, tile)] = x[r, pl.ds(at, tile), :].T

    side = min(256, width)
    slots = ((0, 1), (1, 2), (2, 4), (3, 3))

    def pick(pair, r):
        return pair[0] + r * (pair[1] - pair[0])

    def product(t, r, into):
        slot = pick(slots[t], r)

        @pl.loop(0, width // side)
        def _(i):
            left = pl.multiple_of(i * side, side)
            into[t, :, pl.ds(left, side)] = jnp.dot(
                xt[r], x[slot, :, pl.ds(left, side)], preferred_element_type=jnp.float32
            )

    def gave(t):
        return remote(give.at[t], got.at[t], give_send.at[t], give_recv.at[t], dev(c, 1 - j, s))

    def grams(steps):
        for t, only in steps:
            @pl.when(True if only is None else 1 - j == only)
            def _():
                product(t, 1 - j, give)
                gave(t).start()
        for t, only in steps:
            @pl.when(True if only is None else j == only)
            def _():
                product(t, j, mine)
        for t, only in steps:
            @pl.when(True if only is None else j == only)
            def _():
                gave(t).wait_recv()

    block = width // 2 // SUBS

    def chain(n):
        way = n // SUBS
        u = n % SUBS
        lines = pl.ds(pl.multiple_of(way * (width // 2) + u * block, block), block)
        first = s == way * (ns - 1)
        last = s == (1 - way) * (ns - 1)
        step = 1 - 2 * way
        return lines, first, last, step

    def place(t):
        k = jnp.where((j == 1) & (t >= 2), 5 - t, t)
        return pl.ds(pl.multiple_of(k * width, width), width)

    def to_sum(t, n, group):
        lines = chain(n)[0]
        return remote(mine.at[t, lines, :], arrived.at[t, lines, :], sum_send.at[t, n],
                      sum_recv.at[t, n], dev(c, j, group))

    def to_back(t, n, group):
        lines = chain(n)[0]
        spot = result.at[lines, place(t)]
        return remote(spot, spot, back_send.at[t, n], back_recv.at[t, n], dev(c, j, group))

    def reduce(t, n):
        lines, first, last, step = chain(n)
        mine[t, lines, :] = mine[t, lines, :] + got[t, lines, :]

        @pl.when(jnp.logical_not(first))
        def _():
            to_sum(t, n, s - step).wait_recv()
            mine[t, lines, :] = mine[t, lines, :] + arrived[t, lines, :]

        @pl.when(jnp.logical_not(last))
        def _():
            to_sum(t, n, s + step).start()

        @pl.when(last)
        def _():
            result[lines, place(t)] = (mine[t, lines, :] / total).astype(jnp.bfloat16)
            to_back(t, n, s - step).start()

    def bring(t, n):
        lines, first, last, step = chain(n)

        @pl.when(jnp.logical_not(last))
        def _():
            to_back(t, n, s + step).wait_recv()

            @pl.when(jnp.logical_not(first))
            def _():
                to_back(t, n, s - step).start()

    def walk(start, count, beside=None):
        pieces = count * SUBS
        ends = ns - 1

        @pl.loop(0, pieces + 2 * ends + SLACK)
        def _(turn):
            for way in range(2):
                hops = s if way == 0 else ends - s
                for u, body in (
                    (turn - hops, reduce),
                    (turn - (2 * ends - hops + SLACK), bring),
                ):
                    @pl.when((u >= 0) & (u < pieces))
                    def _():
                        body(start + u // SUBS, way * SUBS + u % SUBS)
            if beside is not None:
                beside(turn)

    def store(t):
        return pltpu.make_async_copy(result.at[:, place(t)], out.at[:, place(t)], out_sem.at[t])

    shortest = SUBS + 2 * (ns - 1) + SLACK
    inside = len([q for q in range(PARTS) if PACE * q + 1 < shortest])

    def beside(turn):
        @pl.when((turn % PACE == 1) & (turn // PACE < inside))
        def _():
            relay(turn // PACE)

    grams(((0, None), (1, 0)))
    walk(0, 2 - j, beside)
    for q in range(inside, PARTS):
        relay(q)
    store(0).start()
    take_near()
    take_far()
    grams(((1, 1), (2, None)))
    walk(2 - j, 1 + j)
    store(1).start()
    store(2).start()
    take_third()
    grams(((3, None),))
    walk(3, 1)
    store(3).start()

    for off in range(1, ns):
        stat_out(off).wait_send()
    swap.wait_send()

    @pl.when(has_far)
    def _():
        for q in range(PARTS):
            far(q).wait_send()

    @pl.when(has_near)
    def _():
        for q in range(PARTS):
            near(q).wait_send()

    @pl.when(c >= 1)
    def _():
        third().wait_send()

    @pl.when(relays)
    def _():
        for q in range(PARTS):
            passed(q).wait_send()

    for t in range(REACH):
        gave(t).wait_send()
        store(t).wait()

        @pl.loop(0, 2 * SUBS)
        def _(n):
            lines, first, last, step = chain(n)

            @pl.when(jnp.logical_not(last))
            def _():
                to_sum(t, n, s + step).wait_send()

            @pl.when(jnp.logical_not(first))
            def _():
                to_back(t, n, s - step).wait_send()


def per_device(nv, ns, dosages, window_end):
    rows, width = dosages.shape
    half = rows // 2
    dma = pltpu.SemaphoreType.DMA
    f32, bf16 = jnp.float32, jnp.bfloat16
    raw = pl.pallas_call(
        functools.partial(kernel, rows * ns, nv, ns),
        out_shape=jax.ShapeDtypeStruct((width, REACH * width), bf16),
        in_specs=[pl.BlockSpec(memory_space=pltpu.VMEM)],
        out_specs=pl.BlockSpec(memory_space=pl.ANY),
        scratch_shapes=[
            pltpu.VMEM((REACH + 1, half, width), bf16),
            pltpu.VMEM((2, width, half), bf16),
            pltpu.VMEM((half, width), bf16),
            pltpu.VMEM((ns, 8, width), f32),
            pltpu.VMEM((REACH, width, width), f32),
            pltpu.VMEM((REACH, width, width), f32),
            pltpu.VMEM((REACH, width, width), f32),
            pltpu.VMEM((REACH, width, width), f32),
            pltpu.VMEM((width, REACH * width), bf16),
            dma((ns,)), dma((ns,)), dma(()), dma(()),
            dma((PARTS,)), dma((PARTS,)), dma((PARTS,)), dma(()),
            dma((PARTS,)), dma((PARTS,)), dma(()), dma((REACH,)), dma((REACH,)),
            dma((REACH, 2 * SUBS)), dma((REACH, 2 * SUBS)),
            dma((REACH, 2 * SUBS)), dma((REACH, 2 * SUBS)), dma((REACH,)),
        ],
        compiler_params=pltpu.CompilerParams(
            collective_id=0, has_side_effects=True, vmem_limit_bytes=60 * 1024 * 1024
        ),
    )(dosages)
    columns = jnp.arange(REACH * width, dtype=jnp.int32)
    target = lax.axis_index("var") * width + columns
    keep = (columns[None, :] < width) | (target[None, :] <= window_end[:, None])
    return jnp.where(keep, raw, jnp.zeros((), bf16))


def solution(mesh):
    placed = (P("samp", "var"), P("var"))
    return jax.shard_map(
        functools.partial(per_device, mesh.shape["var"], mesh.shape["samp"]),
        mesh=mesh, in_specs=placed, out_specs=P("var", None), check_vma=False,
    )
```

```python
import functools

import jax
import jax.numpy as jnp
from jax import lax
from jax.experimental import pallas as pl
from jax.experimental.pallas import tpu as pltpu
from jax.sharding import PartitionSpec as P

MESH = pl.DeviceIdType.MESH
REACH = 4
PARTS = 4
SUBS = 8
SLACK = 4
LAG = 3


def kernel(
    total, nv, ns, data, out, x, xt, other, stat, mine, give, got, arrived, result,
    stat_send, stat_recv, swap_send, swap_recv, near_send, far_send, pass_send, third_send,
    near_recv, far_recv, third_recv, give_send, give_recv,
    sum_send, sum_recv, back_send, back_recv, out_sem,
):
    v = lax.axis_index("var")
    s = lax.axis_index("samp")
    rows, width = data.shape
    half = rows // 2
    chips = nv // 2
    c = v // 2
    j = v % 2
    tile = min(256, half)
    part = half // PARTS

    def dev(chip, core, group):
        return {"var": chip * 2 + core, "samp": group}

    def remote(src, dst, send, recv, where):
        return pltpu.make_async_remote_copy(
            src_ref=src, dst_ref=dst, send_sem=send, recv_sem=recv,
            device_id=where, device_id_type=MESH,
        )

    barrier = pltpu.get_barrier_semaphore()

    def greet(where):
        pl.semaphore_signal(barrier, inc=1, device_id=where, device_id_type=MESH)

    greet(dev(c, 1 - j, s))
    for off in range(1, ns):
        greet(dev(c, j, lax.rem(s + off, ns)))
    for off in (-2, -1, 1, 2):
        @pl.when((c + off >= 0) & (c + off < chips))
        def _():
            greet(dev(c + off, j, s))

    def add_up(i, carry):
        a, b = carry
        d = data[pl.ds(pl.multiple_of(i * tile, tile), tile), :].astype(jnp.float32)
        d = d.reshape(tile // 8, 8, width)
        return a + jnp.sum(d, axis=0), b + jnp.sum(d * d, axis=0)

    zero = jnp.zeros((8, width), jnp.float32)
    a, b = lax.fori_loop(0, rows // tile, add_up, (zero, zero))
    stat[s, 0:1, :] = jnp.sum(a, axis=0, keepdims=True)
    stat[s, 1:2, :] = jnp.sum(b, axis=0, keepdims=True)

    peers = jnp.int32(ns)
    for off in (-2, -1, 1, 2):
        peers = peers + ((c + off >= 0) & (c + off < chips)).astype(jnp.int32)
    pl.semaphore_wait(barrier, peers)

    def stat_out(off):
        return remote(stat.at[s], stat.at[s], stat_send.at[off], stat_recv.at[s],
                      dev(c, j, lax.rem(s + off, ns)))

    for off in range(1, ns):
        stat_out(off).start()
    for off in range(1, ns):
        src = lax.rem(s + off, ns)
        remote(stat.at[src], stat.at[src], stat_send.at[off], stat_recv.at[src],
               dev(c, j, src)).wait_recv()
    sums = stat[0, 0:1, :]
    squares = stat[0, 1:2, :]
    for g in range(1, ns):
        sums = sums + stat[g, 0:1, :]
        squares = squares + stat[g, 1:2, :]
    mean = sums / total
    spread = 1.0 / jnp.sqrt(squares / total - mean * mean + 1e-05)

    def standard(start):
        d = data[pl.ds(pl.multiple_of(start, tile), tile), :].astype(jnp.float32)
        return ((d - mean) * spread).astype(jnp.bfloat16)

    @pl.loop(0, half // tile)
    def _(i):
        at = pl.multiple_of(i * tile, tile)
        other[pl.ds(at, tile), :] = standard((1 - j) * half + at)

    swap = remote(other, x.at[j], swap_send, swap_recv, dev(c, 1 - j, s))
    swap.start()

    @pl.loop(0, half // tile)
    def _(i):
        at = pl.multiple_of(i * tile, tile)
        x[j, pl.ds(at, tile), :] = standard(j * half + at)

    for slot, reach in ((2, 1), (3, 1), (4, 2)):
        @pl.when(c + reach >= chips)
        def _():
            @pl.loop(0, half // tile)
            def _(i):
                at = pl.multiple_of(i * tile, tile)
                x[slot, pl.ds(at, tile), :] = jnp.zeros((tile, width), jnp.bfloat16)

    remote(other, x.at[1 - j], swap_send, swap_recv, dev(c, 1 - j, s)).wait_recv()

    def piece(slot, q):
        return x.at[slot, pl.ds(pl.multiple_of(q * part, part), part), :]

    def near(q):
        return remote(piece(0, q), piece(2, q), near_send.at[q], near_recv.at[q], dev(c - 1, j, s))

    def far(q):
        return remote(piece(0, q), piece(4, q), far_send.at[q], far_recv.at[q], dev(c - 2, j, s))

    def passed(q):
        return remote(piece(4, q), piece(2, q), pass_send.at[q], near_recv.at[q], dev(c + 1, j, s))

    def third():
        return remote(x.at[1], x.at[3], third_send, third_recv, dev(c - 1, j, s))

    odd = c % 2 == 1
    has_far = c >= 2
    has_near = (c >= 1) & odd
    relays = (c % 2 == 0) & (c + 2 < chips)

    @pl.when(has_far)
    def _():
        for q in range(PARTS):
            far(q).start()

    @pl.when(has_near)
    def _():
        for q in range(PARTS):
            near(q).start()

    @pl.when(c >= 1)
    def _():
        third().start()

    def far_here(q):
        return remote(piece(0, q), piece(4, q), far_send.at[q], far_recv.at[q], dev(c + 2, j, s))

    def relay(q):
        @pl.when(relays)
        def _():
            far_here(q).wait_recv()
            passed(q).start()

    def take_far():
        @pl.when((c + 2 < chips) & odd)
        def _():
            for q in range(PARTS):
                far_here(q).wait_recv()

    def take_near():
        @pl.when(c + 1 < chips)
        def _():
            for q in range(PARTS):
                remote(piece(0, q), piece(2, q), near_send.at[q], near_recv.at[q],
                       dev(c + 1, j, s)).wait_recv()

    def take_third():
        @pl.when(c + 1 < chips)
        def _():
            remote(x.at[1], x.at[3], third_send, third_recv, dev(c + 1, j, s)).wait_recv()

    for r in range(2):
        @pl.loop(0, half // tile)
        def _(i):
            at = pl.multiple_of(i * tile, tile)
            xt[r, :, pl.ds(at, tile)] = x[r, pl.ds(at, tile), :].T

    side = min(256, width)
    slots = ((0, 1), (1, 2), (2, 4), (3, 3))

    def pick(pair, r):
        return pair[0] + r * (pair[1] - pair[0])

    def product(t, r, into):
        slot = pick(slots[t], r)

        @pl.loop(0, width // side)
        def _(i):
            left = pl.multiple_of(i * side, side)
            into[t, :, pl.ds(left, side)] = jnp.dot(
                xt[r], x[slot, :, pl.ds(left, side)], preferred_element_type=jnp.float32
            )

    def gave(t):
        return remote(give.at[t], got.at[t], give_send.at[t], give_recv.at[t], dev(c, 1 - j, s))

    def grams(steps):
        for t, only in steps:
            @pl.when(True if only is None else 1 - j == only)
            def _():
                product(t, 1 - j, give)
                gave(t).start()
        for t, only in steps:
            @pl.when(True if only is None else j == only)
            def _():
                product(t, j, mine)
        for t, only in steps:
            @pl.when(True if only is None else j == only)
            def _():
                gave(t).wait_recv()

    block = width // 2 // SUBS

    def chain(n):
        way = n // SUBS
        u = n % SUBS
        lines = pl.ds(pl.multiple_of(way * (width // 2) + u * block, block), block)
        first = s == way * (ns - 1)
        last = s == (1 - way) * (ns - 1)
        step = 1 - 2 * way
        return lines, first, last, step

    def place(t):
        k = jnp.where((j == 1) & (t >= 2), 5 - t, t)
        return pl.ds(pl.multiple_of(k * width, width), width)

    def to_sum(t, n, group):
        lines = chain(n)[0]
        return remote(mine.at[t, lines, :], arrived.at[t, lines, :], sum_send.at[t, n],
                      sum_recv.at[t, n], dev(c, j, group))

    def to_back(t, n, group):
        lines = chain(n)[0]
        spot = result.at[lines, place(t)]
        return remote(spot, spot, back_send.at[t, n], back_recv.at[t, n], dev(c, j, group))

    def reduce(t, n):
        lines, first, last, step = chain(n)
        mine[t, lines, :] = mine[t, lines, :] + got[t, lines, :]

        @pl.when(jnp.logical_not(first))
        def _():
            to_sum(t, n, s - step).wait_recv()
            mine[t, lines, :] = mine[t, lines, :] + arrived[t, lines, :]

        @pl.when(jnp.logical_not(last))
        def _():
            to_sum(t, n, s + step).start()

        @pl.when(last)
        def _():
            result[lines, place(t)] = (mine[t, lines, :] / total).astype(jnp.bfloat16)
            to_back(t, n, s - step).start()

    def bring(t, n):
        lines, first, last, step = chain(n)

        @pl.when(jnp.logical_not(last))
        def _():
            to_back(t, n, s + step).wait_recv()

            @pl.when(jnp.logical_not(first))
            def _():
                to_back(t, n, s - step).start()

    def walk(start, count, beside=None):
        pieces = count * SUBS
        ends = LAG * (ns - 1)

        @pl.loop(0, pieces + 2 * ends + SLACK)
        def _(turn):
            for way in range(2):
                hops = LAG * (s if way == 0 else ns - 1 - s)
                for u, body in (
                    (turn - hops, reduce),
                    (turn - (2 * ends - hops + SLACK), bring),
                ):
                    @pl.when((u >= 0) & (u < pieces))
                    def _():
                        body(start + u // SUBS, way * SUBS + u % SUBS)
            if beside is not None:
                beside(turn)

    def store(t):
        return pltpu.make_async_copy(result.at[:, place(t)], out.at[:, place(t)], out_sem.at[t])

    shortest = SUBS + 2 * LAG * (ns - 1) + SLACK
    pace = max(1, shortest // PARTS)
    inside = len([q for q in range(PARTS) if pace * q < shortest])

    def beside(turn):
        @pl.when((turn % pace == 0) & (turn // pace < inside))
        def _():
            relay(turn // pace)

    grams(((0, None), (1, 0)))
    walk(0, 2 - j, beside)
    for q in range(inside, PARTS):
        relay(q)
    store(0).start()
    take_near()
    grams(((1, 1), (2, 0)))
    walk(2 - j, 1)
    store(1).start()
    take_far()
    take_third()
    grams(((2, 1), (3, None)))
    walk(3 - j, 1 + j)
    store(2).start()
    store(3).start()

    for off in range(1, ns):
        stat_out(off).wait_send()
    swap.wait_send()

    @pl.when(has_far)
    def _():
        for q in range(PARTS):
            far(q).wait_send()

    @pl.when(has_near)
    def _():
        for q in range(PARTS):
            near(q).wait_send()

    @pl.when(c >= 1)
    def _():
        third().wait_send()

    @pl.when(relays)
    def _():
        for q in range(PARTS):
            passed(q).wait_send()

    for t in range(REACH):
        gave(t).wait_send()
        store(t).wait()

        @pl.loop(0, 2 * SUBS)
        def _(n):
            lines, first, last, step = chain(n)

            @pl.when(jnp.logical_not(last))
            def _():
                to_sum(t, n, s + step).wait_send()

            @pl.when(jnp.logical_not(first))
            def _():
                to_back(t, n, s - step).wait_send()


def per_device(nv, ns, dosages, window_end):
    rows, width = dosages.shape
    half = rows // 2
    dma = pltpu.SemaphoreType.DMA
    f32, bf16 = jnp.float32, jnp.bfloat16
    raw = pl.pallas_call(
        functools.partial(kernel, rows * ns, nv, ns),
        out_shape=jax.ShapeDtypeStruct((width, REACH * width), bf16),
        in_specs=[pl.BlockSpec(memory_space=pltpu.VMEM)],
        out_specs=pl.BlockSpec(memory_space=pl.ANY),
        scratch_shapes=[
            pltpu.VMEM((REACH + 1, half, width), bf16),
            pltpu.VMEM((2, width, half), bf16),
            pltpu.VMEM((half, width), bf16),
            pltpu.VMEM((ns, 8, width), f32),
            pltpu.VMEM((REACH, width, width), f32),
            pltpu.VMEM((REACH, width, width), f32),
            pltpu.VMEM((REACH, width, width), f32),
            pltpu.VMEM((REACH, width, width), f32),
            pltpu.VMEM((width, REACH * width), bf16),
            dma((ns,)), dma((ns,)), dma(()), dma(()),
            dma((PARTS,)), dma((PARTS,)), dma((PARTS,)), dma(()),
            dma((PARTS,)), dma((PARTS,)), dma(()), dma((REACH,)), dma((REACH,)),
            dma((REACH, 2 * SUBS)), dma((REACH, 2 * SUBS)),
            dma((REACH, 2 * SUBS)), dma((REACH, 2 * SUBS)), dma((REACH,)),
        ],
        compiler_params=pltpu.CompilerParams(
            collective_id=0, has_side_effects=True, vmem_limit_bytes=60 * 1024 * 1024
        ),
    )(dosages)
    columns = jnp.arange(REACH * width, dtype=jnp.int32)
    target = lax.axis_index("var") * width + columns
    keep = (columns[None, :] < width) | (target[None, :] <= window_end[:, None])
    return jnp.where(keep, raw, jnp.zeros((), bf16))


def solution(mesh):
    placed = (P("samp", "var"), P("var"))
    return jax.shard_map(
        functools.partial(per_device, mesh.shape["var"], mesh.shape["samp"]),
        mesh=mesh, in_specs=placed, out_specs=P("var", None), check_vma=False,
    )
```

```python
import functools

import jax
import jax.numpy as jnp
from jax import lax
from jax.experimental import pallas as pl
from jax.experimental.pallas import tpu as pltpu
from jax.sharding import PartitionSpec as P

MESH = pl.DeviceIdType.MESH
REACH = 4
PARTS = 4
SUBS = 8
SLACK = 4
LAG = 3


def kernel(
    total, nv, ns, data, out, x, xt, other, stat, mine, give, got, arrived, result,
    stat_send, stat_recv, swap_send, swap_recv, near_send, far_send, pass_send, third_send,
    near_recv, far_recv, third_recv, give_send, give_recv,
    sum_send, sum_recv, back_send, back_recv, out_sem,
):
    v = lax.axis_index("var")
    s = lax.axis_index("samp")
    rows, width = data.shape
    half = rows // 2
    chips = nv // 2
    c = v // 2
    j = v % 2
    tile = min(256, half)
    part = half // PARTS

    def dev(chip, core, group):
        return {"var": chip * 2 + core, "samp": group}

    def remote(src, dst, send, recv, where):
        return pltpu.make_async_remote_copy(
            src_ref=src, dst_ref=dst, send_sem=send, recv_sem=recv,
            device_id=where, device_id_type=MESH,
        )

    barrier = pltpu.get_barrier_semaphore()

    def greet(where):
        pl.semaphore_signal(barrier, inc=1, device_id=where, device_id_type=MESH)

    greet(dev(c, 1 - j, s))
    for off in range(1, ns):
        greet(dev(c, j, lax.rem(s + off, ns)))
    for off in (-2, -1, 1, 2):
        @pl.when((c + off >= 0) & (c + off < chips))
        def _():
            greet(dev(c + off, j, s))

    def add_up(i, carry):
        a, b = carry
        d = data[pl.ds(pl.multiple_of(i * tile, tile), tile), :].astype(jnp.float32)
        d = d.reshape(tile // 8, 8, width)
        return a + jnp.sum(d, axis=0), b + jnp.sum(d * d, axis=0)

    zero = jnp.zeros((8, width), jnp.float32)
    a, b = lax.fori_loop(0, rows // tile, add_up, (zero, zero))
    stat[s, 0:1, :] = jnp.sum(a, axis=0, keepdims=True)
    stat[s, 1:2, :] = jnp.sum(b, axis=0, keepdims=True)

    peers = jnp.int32(ns)
    for off in (-2, -1, 1, 2):
        peers = peers + ((c + off >= 0) & (c + off < chips)).astype(jnp.int32)
    pl.semaphore_wait(barrier, peers)

    def stat_out(off):
        return remote(stat.at[s], stat.at[s], stat_send.at[off], stat_recv.at[s],
                      dev(c, j, lax.rem(s + off, ns)))

    for off in range(1, ns):
        stat_out(off).start()
    for off in range(1, ns):
        src = lax.rem(s + off, ns)
        remote(stat.at[src], stat.at[src], stat_send.at[off], stat_recv.at[src],
               dev(c, j, src)).wait_recv()
    sums = stat[0, 0:1, :]
    squares = stat[0, 1:2, :]
    for g in range(1, ns):
        sums = sums + stat[g, 0:1, :]
        squares = squares + stat[g, 1:2, :]
    mean = sums / total
    spread = 1.0 / jnp.sqrt(squares / total - mean * mean + 1e-05)

    def standard(start):
        d = data[pl.ds(pl.multiple_of(start, tile), tile), :].astype(jnp.float32)
        return ((d - mean) * spread).astype(jnp.bfloat16)

    @pl.loop(0, half // tile)
    def _(i):
        at = pl.multiple_of(i * tile, tile)
        other[pl.ds(at, tile), :] = standard((1 - j) * half + at)

    swap = remote(other, x.at[j], swap_send, swap_recv, dev(c, 1 - j, s))
    swap.start()

    @pl.loop(0, half // tile)
    def _(i):
        at = pl.multiple_of(i * tile, tile)
        x[j, pl.ds(at, tile), :] = standard(j * half + at)

    def piece(slot, q):
        return x.at[slot, pl.ds(pl.multiple_of(q * part, part), part), :]

    def near(q):
        return remote(piece(0, q), piece(2, q), near_send.at[q], near_recv.at[q], dev(c - 1, j, s))

    def far(q):
        return remote(piece(0, q), piece(4, q), far_send.at[q], far_recv.at[q], dev(c - 2, j, s))

    def passed(q):
        return remote(piece(4, q), piece(2, q), pass_send.at[q], near_recv.at[q], dev(c + 1, j, s))

    def third():
        return remote(x.at[1], x.at[3], third_send, third_recv, dev(c - 1, j, s))

    odd = c % 2 == 1
    has_far = c >= 2
    has_near = (c >= 1) & odd
    relays = (c % 2 == 0) & (c + 2 < chips)

    def first_block(core):
        @pl.when(has_far & (j == core))
        def _():
            for q in range(PARTS):
                far(q).start()

        @pl.when(has_near & (j == core))
        def _():
            for q in range(PARTS):
                near(q).start()

    first_block(0)
    remote(other, x.at[1 - j], swap_send, swap_recv, dev(c, 1 - j, s)).wait_recv()

    first_block(1)

    @pl.when(c >= 1)
    def _():
        third().start()

    for slot, reach in ((2, 1), (3, 1), (4, 2)):
        @pl.when(c + reach >= chips)
        def _():
            @pl.loop(0, half // tile)
            def _(i):
                at = pl.multiple_of(i * tile, tile)
                x[slot, pl.ds(at, tile), :] = jnp.zeros((tile, width), jnp.bfloat16)

    def far_here(q):
        return remote(piece(0, q), piece(4, q), far_send.at[q], far_recv.at[q], dev(c + 2, j, s))

    def relay(q):
        @pl.when(relays)
        def _():
            far_here(q).wait_recv()
            passed(q).start()

    def take_far():
        @pl.when((c + 2 < chips) & odd)
        def _():
            for q in range(PARTS):
                far_here(q).wait_recv()

    def take_near():
        @pl.when(c + 1 < chips)
        def _():
            for q in range(PARTS):
                remote(piece(0, q), piece(2, q), near_send.at[q], near_recv.at[q],
                       dev(c + 1, j, s)).wait_recv()

    def take_third():
        @pl.when(c + 1 < chips)
        def _():
            remote(x.at[1], x.at[3], third_send, third_recv, dev(c + 1, j, s)).wait_recv()

    for r in range(2):
        @pl.loop(0, half // tile)
        def _(i):
            at = pl.multiple_of(i * tile, tile)
            xt[r, :, pl.ds(at, tile)] = x[r, pl.ds(at, tile), :].T

    side = min(256, width)
    slots = ((0, 1), (1, 2), (2, 4), (3, 3))

    def pick(pair, r):
        return pair[0] + r * (pair[1] - pair[0])

    def product(t, r, into):
        slot = pick(slots[t], r)

        @pl.loop(0, width // side)
        def _(i):
            left = pl.multiple_of(i * side, side)
            into[t, :, pl.ds(left, side)] = jnp.dot(
                xt[r], x[slot, :, pl.ds(left, side)], preferred_element_type=jnp.float32
            )

    def gave(t):
        return remote(give.at[t], got.at[t], give_send.at[t], give_recv.at[t], dev(c, 1 - j, s))

    def grams(steps):
        for t, only in steps:
            @pl.when(True if only is None else 1 - j == only)
            def _():
                product(t, 1 - j, give)
                gave(t).start()
        for t, only in steps:
            @pl.when(True if only is None else j == only)
            def _():
                product(t, j, mine)
        for t, only in steps:
            @pl.when(True if only is None else j == only)
            def _():
                gave(t).wait_recv()

    block = width // 2 // SUBS

    def chain(n):
        way = n // SUBS
        u = n % SUBS
        lines = pl.ds(pl.multiple_of(way * (width // 2) + u * block, block), block)
        first = s == way * (ns - 1)
        last = s == (1 - way) * (ns - 1)
        step = 1 - 2 * way
        return lines, first, last, step

    def place(t):
        k = jnp.where((j == 1) & (t >= 2), 5 - t, t)
        return pl.ds(pl.multiple_of(k * width, width), width)

    def to_sum(t, n, group):
        lines = chain(n)[0]
        return remote(mine.at[t, lines, :], arrived.at[t, lines, :], sum_send.at[t, n],
                      sum_recv.at[t, n], dev(c, j, group))

    def to_back(t, n, group):
        lines = chain(n)[0]
        spot = result.at[lines, place(t)]
        return remote(spot, spot, back_send.at[t, n], back_recv.at[t, n], dev(c, j, group))

    def reduce(t, n):
        lines, first, last, step = chain(n)
        mine[t, lines, :] = mine[t, lines, :] + got[t, lines, :]

        @pl.when(jnp.logical_not(first))
        def _():
            to_sum(t, n, s - step).wait_recv()
            mine[t, lines, :] = mine[t, lines, :] + arrived[t, lines, :]

        @pl.when(jnp.logical_not(last))
        def _():
            to_sum(t, n, s + step).start()

        @pl.when(last)
        def _():
            result[lines, place(t)] = (mine[t, lines, :] / total).astype(jnp.bfloat16)
            to_back(t, n, s - step).start()

    def bring(t, n):
        lines, first, last, step = chain(n)

        @pl.when(jnp.logical_not(last))
        def _():
            to_back(t, n, s + step).wait_recv()

            @pl.when(jnp.logical_not(first))
            def _():
                to_back(t, n, s - step).start()

    def walk(start, count, beside=None):
        pieces = count * SUBS
        ends = LAG * (ns - 1)

        @pl.loop(0, pieces + 2 * ends + SLACK)
        def _(turn):
            for way in range(2):
                hops = LAG * (s if way == 0 else ns - 1 - s)
                for u, body in (
                    (turn - hops, reduce),
                    (turn - (2 * ends - hops + SLACK), bring),
                ):
                    @pl.when((u >= 0) & (u < pieces))
                    def _():
                        body(start + u // SUBS, way * SUBS + u % SUBS)
            if beside is not None:
                beside(turn)

    def store(t):
        return pltpu.make_async_copy(result.at[:, place(t)], out.at[:, place(t)], out_sem.at[t])

    shortest = SUBS + 2 * LAG * (ns - 1) + SLACK
    pace = max(1, shortest // PARTS)
    inside = len([q for q in range(PARTS) if pace * q < shortest])

    def beside(turn):
        @pl.when((turn % pace == 0) & (turn // pace < inside))
        def _():
            relay(turn // pace)

    grams(((0, None), (1, 0)))
    walk(0, 2 - j, beside)
    for q in range(inside, PARTS):
        relay(q)
    store(0).start()
    take_near()
    grams(((1, 1), (2, 0)))
    walk(2 - j, 1)
    store(1).start()
    take_far()
    take_third()
    grams(((2, 1), (3, None)))
    walk(3 - j, 1 + j)
    store(2).start()
    store(3).start()

    for off in range(1, ns):
        stat_out(off).wait_send()
    swap.wait_send()

    @pl.when(has_far)
    def _():
        for q in range(PARTS):
            far(q).wait_send()

    @pl.when(has_near)
    def _():
        for q in range(PARTS):
            near(q).wait_send()

    @pl.when(c >= 1)
    def _():
        third().wait_send()

    @pl.when(relays)
    def _():
        for q in range(PARTS):
            passed(q).wait_send()

    for t in range(REACH):
        gave(t).wait_send()
        store(t).wait()

        @pl.loop(0, 2 * SUBS)
        def _(n):
            lines, first, last, step = chain(n)

            @pl.when(jnp.logical_not(last))
            def _():
                to_sum(t, n, s + step).wait_send()

            @pl.when(jnp.logical_not(first))
            def _():
                to_back(t, n, s - step).wait_send()


def per_device(nv, ns, dosages, window_end):
    rows, width = dosages.shape
    half = rows // 2
    dma = pltpu.SemaphoreType.DMA
    f32, bf16 = jnp.float32, jnp.bfloat16
    raw = pl.pallas_call(
        functools.partial(kernel, rows * ns, nv, ns),
        out_shape=jax.ShapeDtypeStruct((width, REACH * width), bf16),
        in_specs=[pl.BlockSpec(memory_space=pltpu.VMEM)],
        out_specs=pl.BlockSpec(memory_space=pl.ANY),
        scratch_shapes=[
            pltpu.VMEM((REACH + 1, half, width), bf16),
            pltpu.VMEM((2, width, half), bf16),
            pltpu.VMEM((half, width), bf16),
            pltpu.VMEM((ns, 8, width), f32),
            pltpu.VMEM((REACH, width, width), f32),
            pltpu.VMEM((REACH, width, width), f32),
            pltpu.VMEM((REACH, width, width), f32),
            pltpu.VMEM((REACH, width, width), f32),
            pltpu.VMEM((width, REACH * width), bf16),
            dma((ns,)), dma((ns,)), dma(()), dma(()),
            dma((PARTS,)), dma((PARTS,)), dma((PARTS,)), dma(()),
            dma((PARTS,)), dma((PARTS,)), dma(()), dma((REACH,)), dma((REACH,)),
            dma((REACH, 2 * SUBS)), dma((REACH, 2 * SUBS)),
            dma((REACH, 2 * SUBS)), dma((REACH, 2 * SUBS)), dma((REACH,)),
        ],
        compiler_params=pltpu.CompilerParams(
            collective_id=0, has_side_effects=True, vmem_limit_bytes=60 * 1024 * 1024
        ),
    )(dosages)
    columns = jnp.arange(REACH * width, dtype=jnp.int32)
    target = lax.axis_index("var") * width + columns
    keep = (columns[None, :] < width) | (target[None, :] <= window_end[:, None])
    return jnp.where(keep, raw, jnp.zeros((), bf16))


def solution(mesh):
    placed = (P("samp", "var"), P("var"))
    return jax.shard_map(
        functools.partial(per_device, mesh.shape["var"], mesh.shape["samp"]),
        mesh=mesh, in_specs=placed, out_specs=P("var", None), check_vma=False,
    )
```
